32 devices in a mesh: seq: 2 (over x), hist: 8 (over z, y), chan: 2 (over core).
Axes of the slice: x: 2, y: 2, z: 4, core: 2. Of those that a mesh axis runs over, the one named last changes fastest.
Arguments:
- history: bfloat16 [4096, 4096], P(('seq', 'hist'), 'chan'), parts along dimension 0, may hold values from -6 to 6
- filter_taps: bfloat16 [2048, 4096], P('hist', 'chan'), may hold values from -0.125 to 0.125
- gate_values: bfloat16 [512, 4096], P(('seq', 'hist'), 'chan'), parts along dimension 0, may hold values from -6 to 6
- out_weight: bfloat16 [4096, 4096], P('chan', 'hist'), may hold values from -0.09375 to 0.09375
Outputs:
- output: bfloat16 [512, 4096], P(('seq', 'hist', 'chan')), parts along dimension 0
The draws below stay inside these ranges and needn't reach their ends.
There are 2 independent parts, one for each index of `seq`. The reference program is written for one: setup_inputs(seed, part) draws one part's arguments, and reference() takes and returns one part's arrays. A program takes and returns all parts, laid end to end along the dimension named above; an argument that names none is the same for every part. Nothing has to cross between parts.
All inputs are finite; a program needn't handle non-finite values.
Results may differ from the reference program's by a relative error of at most 0.013.
Values may be sent and summed in bfloat16 or wider, within the bound.
A program may use at most 64 MiB of HBM per device.

```python
import jax
import jax.numpy as jnp
from jax import lax

D = 4096
TB = 256
HIST = 2048


def level_of(own_key, shape, split, low, largest):
    factor_of = 1.0
    for dim, parts in split:
        steps = jax.random.uniform(jax.random.fold_in(jax.random.fold_in(own_key, 6), dim), (parts,), jnp.float32, low / len(split), largest / len(split))
        factor_of = factor_of * jnp.repeat(jnp.exp(steps), shape[dim] // parts).reshape((-1,) + (1,) * (len(shape) - 1 - dim))
    return factor_of


def centred(rng, extent, width, bound, pieces=(), dtype=jnp.bfloat16):
    values = jax.random.normal(rng, extent, jnp.float32) * width
    if len(pieces) > 0:
        values = level_of(rng, extent, pieces, -0.22, 0.18) * values
    return jnp.clip(values, min=-bound, max=bound).astype(dtype)


def setup_inputs(seed: int = 0, part: int = 0) -> dict:
    keys = jax.random.split(jax.random.key(seed), 5)
    part_keys = jax.random.split(jax.random.fold_in(keys[4], part), 5)
    history = centred(part_keys[0], (HIST, D), 1.0, 6.0, ((0, 8), (1, 2)))
    filter_taps = centred(keys[1], (HIST, D), (HIST ** -0.5), 0.125, ((0, 8), (1, 2)))
    gate_values = centred(part_keys[2], (TB, D), 1.0, 6.0, ((0, 8), (1, 2)))
    out_weight = centred(keys[3], (D, D), D ** -0.5, 0.09375, ((0, 2), (1, 8)))
    return dict(history=history, filter_taps=filter_taps, gate_values=gate_values, out_weight=out_weight)


def reference(history, filter_taps, gate_values, out_weight):
    block_width = min(256, D)
    count_blocks = D // block_width
    signal = history.astype(jnp.float32).reshape(HIST, count_blocks, block_width).transpose(1, 0, 2)
    kernel = filter_taps.astype(jnp.float32)[::-1].reshape(HIST, count_blocks, block_width).transpose(1, 0, 2)
    length = 2 * HIST

    def conv_block(pair):
        inputs, taps_block = pair
        spectrum = jnp.fft.rfft(inputs, length, axis=0) * jnp.fft.rfft(taps_block, length, axis=0)
        whole = jnp.fft.irfft(spectrum, length, axis=0)
        return whole[HIST - TB:HIST]

    blocks = lax.map(conv_block, (signal, kernel))
    conv = blocks.transpose(1, 0, 2).reshape(TB, D).astype(jnp.float32)
    gated = (conv * gate_values.astype(jnp.float32)).astype(jnp.bfloat16)
    return jnp.dot(gated, out_weight, preferred_element_type=jnp.float32).astype(jnp.bfloat16)
```

```python
import functools
import math

import jax
import jax.numpy as jnp
import numpy as np
from jax import lax
from jax.experimental import pallas as pl
from jax.experimental.pallas import tpu as pltpu
from jax.sharding import PartitionSpec as P

MESH = pl.DeviceIdType.MESH
BF16 = jnp.bfloat16
F32 = jnp.float32
LANES = 128
PARTS = (1, 1, 1, 1)
LAST = (3, 0)
DIRECT = ()
SLANT = ((2, 0), (3, 1), (3, 0))
ISSUE = (
    (
        "h", "t0", "t1", "y0", "t2", "t3", "y1", "y2", "y3", "x0",
    ),
    (
        "g", "x1", "d0", "x2", "x3",
    ),
    (
        "d1",
    ),
    (
        "d2",
    ),
    (
        "d3",
    ),
)
EVENTS = (
    "r0", "g", "r1", "c00", "m1", "r2", "c01", "m2", "r3", "p", "n00", "c11", "n01", "c10", "m3",
    "c21", "d00", "n11", "d01", "c20", "c31", "n10", "c30", "n21", "d11", "n20", "d10", "n31", "d21",
    "n30", "d20", "d31", "d30", "f00", "f01", "f11", "f10", "f21", "f20", "f31", "f30", "j00", "j01",
    "j11", "j10", "j21", "j20", "j31", "j30",
)


def tables(local_rows, block_tokens):
    period = local_rows + block_tokens
    modes = period // 2
    odd = 2 * np.arange(modes) + 1
    turn = math.pi / period
    places = np.arange(period)
    phase = (np.outer(odd, places) % (2 * period)) * turn
    forward = np.concatenate([np.cos(phase), np.sin(phase)], 0)
    lags = block_tokens - 1 - np.arange(block_tokens)
    phase = (np.outer(lags, odd) % (2 * period)) * turn
    inverse = np.concatenate([np.cos(phase), -np.sin(phase)], 1) * (2.0 / period)
    return forward, inverse


def spectrum_product(taps, values):
    half = taps.shape[0] // 2
    tc, ts, vc, vs = taps[:half], taps[half:], values[:half], values[half:]
    return tc * vc + ts * vs, tc * vs - ts * vc


def dot(a, b):
    return jnp.dot(a, b, preferred_element_type=F32)


def local_general(history, filter_taps, gate_values, out_weight):
    local_rows, channels = history.shape
    owned_rows = gate_values.shape[0]
    count_hist = lax.axis_size("hist")
    count_chan = lax.axis_size("chan")
    block_tokens = owned_rows * count_hist
    forward, inverse = tables(local_rows, block_tokens)
    forward = jnp.asarray(forward, F32)
    forward_high = forward.astype(BF16)
    forward_low = (forward - forward_high.astype(F32)).astype(BF16)
    inverse = jnp.asarray(inverse, F32)
    next_taps = lax.ppermute(
        filter_taps, "hist", [(source, source - 1) for source in range(1, count_hist)]
    )
    extended = jnp.concatenate([filter_taps, next_taps], 0)[: forward.shape[1]]
    spec_taps = dot(forward_high, extended) + dot(forward_low, extended)
    spec_input = dot(forward_high[:, :local_rows], history) + dot(
        forward_low[:, :local_rows], history
    )
    spectrum = jnp.concatenate(spectrum_product(spec_taps, spec_input), 0)
    partial_conv = jnp.dot(
        inverse, spectrum, precision=lax.Precision.HIGHEST, preferred_element_type=F32
    )
    conv = lax.psum_scatter(partial_conv, "hist", scatter_dimension=0, tiled=True)
    gated = (conv * gate_values.astype(F32)).astype(BF16)
    partial_value = dot(lax.all_gather(gated, "hist", axis=0, tiled=True), out_weight)
    columns = partial_value.shape[1]
    half_rows = owned_rows // count_chan
    ordered = partial_value.reshape(count_hist, count_chan, half_rows, columns)
    ordered = ordered.transpose(1, 0, 2, 3).reshape(-1, columns)
    summed = lax.psum_scatter(ordered.astype(BF16), "chan", scatter_dimension=0, tiled=True)
    return lax.all_to_all(summed, "hist", split_axis=0, concat_axis=1, tiled=True)


def nearest(p, k, pairs):
    low = jnp.minimum(p, pairs - 1 - p)
    spot = jnp.where(k <= 2 * low, jnp.where(k % 2 == 1, low - (k + 1) // 2, low + k // 2), k)
    return jnp.where(p * 2 < pairs, spot, pairs - 1 - spot)


def kernel(
    pairs, widths, hist_ref, taps_ref, gate_ref, weight_ref, fwd_ref, inv_ref, out_ref,
    tb, hb, gb, wb, fb, ib, spec_buf, send_buf, own_buf, near_buf, far_buf, stage, gated, acc_buf,
    fin_buf, load_sem, sent, ty_r, hy_r, hx_r, hd_r, zt_r, gate_r, gz_r, wx_r, near_r, far_r, own_r,
    other_r, fin_r, ready_sem,
):
    me = lax.axis_index("hist")
    core = lax.axis_index("chan")
    seq = lax.axis_index("seq")
    p = me // 2
    q = me % 2
    total = 2 * pairs
    rows = hist_ref.shape[0]
    quarter = hist_ref.shape[1] // 4
    half = 2 * quarter
    columns = weight_ref.shape[1]
    partner = 2 * p + (1 - q)
    modes = fb.shape[0] // 2
    across = {"hist": partner}
    beyond = {"seq": 1 - seq}
    diagonal = {"hist": partner, "seq": 1 - seq}
    below = {"hist": jnp.maximum(me - 2, 0)}
    starts = [sum(widths[:i]) for i in range(len(widths) + 1)]
    chunks = range(len(widths))
    middle = (p > 0) & (p < pairs - 1)
    inner = jnp.where(p < 2, 1, 2)
    outer = jnp.where(p < 2, 0, 3)
    to_inner = {"hist": 2 * inner + q}
    to_facing = {"hist": 2 * (3 - inner) + q}

    def remote(src, dst, send, recv, where):
        return pltpu.make_async_remote_copy(
            src_ref=src, dst_ref=dst, send_sem=send, recv_sem=recv,
            device_id=where, device_id_type=MESH,
        )

    def start(src, dst, send, recv, where):
        remote(src, dst, sent.at[send], recv, where).start()

    def arrived(dst, recv):
        remote(dst, dst, load_sem.at[0], recv, {"chan": 1 - core}).wait_recv()

    def drained(src, send):
        remote(src, src, sent.at[send], load_sem.at[0], {"chan": 1 - core}).wait_send()

    def greet(sem, where):
        pl.semaphore_signal(sem, inc=1, device_id=where, device_id_type=MESH)

    def greet_line(sem):
        @pl.when(p > 0)
        def _():
            greet(sem, {"hist": me - 2})

        @pl.when(p < pairs - 1)
        def _():
            greet(sem, {"hist": me + 2})

    barrier = pltpu.get_barrier_semaphore()
    beside = jnp.minimum(p, 1) + jnp.minimum(pairs - 1 - p, 1)
    greet(barrier, across)
    greet_line(barrier)
    greet(barrier, beyond)
    greet(barrier, {"chan": 1 - core})

    def channels(y, x, at=0, width=quarter):
        return pl.ds(pl.multiple_of(y * half + x * quarter + at, LANES), width)

    mine = channels(q, seq)
    loads = [
        pltpu.make_async_copy(taps_ref.at[:, mine], tb.at[q], load_sem.at[0]),
        pltpu.make_async_copy(hist_ref.at[:, mine], hb.at[q, 0], load_sem.at[1]),
        pltpu.make_async_copy(fwd_ref, fb, load_sem.at[2]),
        pltpu.make_async_copy(inv_ref, ib, load_sem.at[3]),
        pltpu.make_async_copy(gate_ref.at[:, mine], gb.at[p, q, 0], load_sem.at[4]),
        pltpu.make_async_copy(weight_ref, wb.at[core], load_sem.at[5]),
    ]
    for copy in loads:
        copy.start()

    @pl.when(p == pairs - 1)
    def _():
        tb[2] = jnp.zeros(tb.shape[1:], BF16)

    pl.semaphore_wait(barrier, 3 + beside)

    def cols(ch):
        return pl.ds(starts[ch], widths[ch])

    def from_hbm(ref, y, x, ch):
        return ref.at[:, channels(y, x, starts[ch], widths[ch])]

    def issue(entry):
        kind = entry[0]
        if kind == "g":
            start(gate_ref.at[:, channels(q, 1 - seq)], gb.at[p, q, 1], 0, gate_r.at[0], beyond)
            start(gate_ref.at[:, channels(1 - q, 1 - seq)], gb.at[p, q, 1], 1, gate_r.at[1], diagonal)
            return
        if kind == "h":
            start(gate_ref.at[:, channels(1 - q, seq)], gb.at[p, q, 0], 2, gate_r.at[2], across)
            return
        ch = int(entry[1:])
        c = cols(ch)
        if kind == "t":
            start(from_hbm(taps_ref, 1 - q, seq, ch), tb.at[q, :, c], 3, ty_r.at[ch], across)
        if kind == "y":
            start(from_hbm(hist_ref, 1 - q, seq, ch), hb.at[q, 0, :, c], 4, hy_r.at[ch], across)
        if kind == "x":
            start(from_hbm(hist_ref, q, 1 - seq, ch), hb.at[q, 1, :, c], 5, hx_r.at[ch], beyond)
        if kind == "d":
            start(from_hbm(hist_ref, 1 - q, 1 - seq, ch), hb.at[q, 1, :, c], 6, hd_r.at[ch], diagonal)

    for entry in ISSUE[0]:
        issue(entry)
    for ch in chunks:
        @pl.when((q == 0) & (p > 0))
        def _():
            start(from_hbm(taps_ref, 0, seq, ch), tb.at[2, :, cols(ch)], 7, zt_r.at[ch], below)

    for r in range(pairs - 2):
        greet_line(ready_sem.at[r])
        if r == 0:
            greet(ready_sem.at[r], across)
            pl.semaphore_wait(ready_sem.at[r], beside + 1)
            for entry in ISSUE[1]:
                issue(entry)
        else:
            pl.semaphore_wait(ready_sem.at[r], beside)
    wx = remote(weight_ref, wb.at[core], sent.at[8], wx_r, {"chan": 1 - core})
    wx.start()

    def more(i):
        for entry in ISSUE[i + 1]:
            issue(entry)

    def relay(ch):
        c = cols(ch)
        arrived(tb.at[1 - q, :, c], ty_r.at[ch])

        @pl.when((q == 1) & (p > 0))
        def _():
            start(tb.at[0, :, c], tb.at[2, :, c], 7, zt_r.at[ch], below)

    once = set()

    def compute(ch, o):
        if "load" not in once:
            for copy in loads[:4]:
                copy.wait()
            once.add("load")
        c = cols(ch)
        width = widths[ch]
        first, second = fb[:, :rows], fb[:, rows:]
        if ("taps", ch) not in once:
            once.add(("taps", ch))

            @pl.when(p < pairs - 1)
            def _():
                arrived(tb.at[2, :, c], zt_r.at[ch])

            t1 = tb[1, :, c]
            spec_buf[ch] = dot(first, jnp.concatenate([tb[0, :, c], t1], 1)) + dot(
                second, jnp.concatenate([t1, tb[2, :, c]], 1)
            )
        if o == 0:
            arrived(hb.at[1 - q, 0, :, c], hy_r.at[ch])
        else:
            arrived(hb.at[q, 1, :, c], hx_r.at[ch])
            arrived(hb.at[1 - q, 1, :, c], hd_r.at[ch])
        values = dot(first, jnp.concatenate([hb[0, o, :, c], hb[1, o, :, c]], 1))
        real, imag = spectrum_product(spec_buf[ch], values)
        real = (real[:, :width] + real[:, width:]).astype(BF16)
        imag = (imag[:, :width] + imag[:, width:]).astype(BF16)
        conv = dot(ib[:, :modes], real) + dot(ib[:, modes:], imag)
        direct = (ch, o) in DIRECT
        if direct:
            send_buf[o, :, c] = conv.astype(BF16)
            own_buf[o, :, c] = conv

            @pl.when(middle)
            def _():
                start(send_buf.at[o, :, c], far_buf.at[0, o, :, c], 9, far_r.at[ch, o], to_facing)

            @pl.when(jnp.logical_not(middle))
            def _():
                start(send_buf.at[o, :, c], far_buf.at[1, o, :, c], 10, far_r.at[ch, o], to_facing)
                start(send_buf.at[o, :, c], near_buf.at[o, :, c], 9, near_r.at[ch, o], to_inner)
        else:
            @pl.when(middle)
            def _():
                own_buf[o, :, c] = conv

            @pl.when(jnp.logical_not(middle))
            def _():
                send_buf[o, :, c] = conv.astype(BF16)
                start(send_buf.at[o, :, c], near_buf.at[o, :, c], 9, near_r.at[ch, o], to_inner)

    def gates():
        loads[4].wait()
        arrived(gb.at[p, 1 - q, 0], gate_r.at[2])
        arrived(gb.at[p, q, 1], gate_r.at[0])
        arrived(gb.at[p, 1 - q, 1], gate_r.at[1])

        @pl.when(middle)
        def _():
            start(gb.at[p], gb.at[p], 19, gz_r.at[1], to_facing)

        @pl.when(jnp.logical_not(middle))
        def _():
            start(gb.at[p], gb.at[p], 19, gz_r.at[0], to_inner)

    def pass_gates():
        @pl.when(middle)
        def _():
            arrived(gb.at[outer], gz_r.at[0])
            start(gb.at[outer], gb.at[outer], 20, gz_r.at[2], to_facing)

    def gather_near(ch, o):
        c = cols(ch)

        @pl.when(middle)
        def _():
            arrived(near_buf.at[o, :, c], near_r.at[ch, o])
            value = own_buf[o, :, c] + near_buf[o, :, c].astype(F32)
            own_buf[o, :, c] = value
            if (ch, o) not in DIRECT:
                send_buf[o, :, c] = value.astype(BF16)
                start(send_buf.at[o, :, c], far_buf.at[0, o, :, c], 9, far_r.at[ch, o], to_facing)

    def reduce(ch, o):
        c = cols(ch)
        width = widths[ch]
        first_time = "gates" not in once
        once.add("gates")

        @pl.when(middle)
        def _():
            if first_time:
                arrived(gb.at[3 - inner], gz_r.at[1])
                arrived(gb.at[3 - outer], gz_r.at[2])
            if (ch, o) in DIRECT:
                arrived(far_buf.at[:, o, :, c], far_r.at[ch, o])
                value = own_buf[o, :, c] + far_buf[0, o, :, c].astype(F32)
                value = value + far_buf[1, o, :, c].astype(F32)
            else:
                arrived(far_buf.at[0, o, :, c], far_r.at[ch, o])
                value = own_buf[o, :, c] + far_buf[0, o, :, c].astype(F32)
            gate = gb[:, :, o, :, c].astype(F32).reshape(value.shape)
            block = (value * gate).astype(BF16).reshape(total, 2, -1, width)
            for kappa in range(2):
                stage[kappa, o, :, c] = block[:, kappa].reshape(-1, width)
            there = gated.at[q, o, core, :, c]
            plane = seq if o == 0 else 1 - seq
            for kappa in range(2):
                start(stage.at[kappa, o, :, c], there, 11, own_r.at[ch, o],
                      {"hist": 2 * outer + q, "seq": plane, "chan": kappa})
            if (ch, o) in SLANT:
                for kappa in range(2):
                    start(stage.at[kappa, o, :, c], there, 15, other_r.at[ch, o],
                          {"hist": 2 * outer + 1 - q, "seq": plane, "chan": kappa})
            for kappa in range(2):
                start(stage.at[kappa, o, :, c], there, 12, other_r.at[ch, o],
                      {"hist": partner, "seq": plane, "chan": kappa})
            if o == 1:
                for kappa in range(2):
                    start(stage.at[kappa, o, :, c], there, 13, own_r.at[ch, o],
                          {"seq": plane, "chan": kappa})
            else:
                start(stage.at[1 - core, o, :, c], there, 14, own_r.at[ch, o], {"chan": 1 - core})
                gated[q, o, core, :, c] = stage[core, o, :, c]

    def forward(ch, o):
        c = cols(ch)
        block = gated.at[q, o, :, :, c]

        @pl.when(jnp.logical_not(middle))
        def _():
            arrived(block, own_r.at[ch, o])
            if (ch, o) not in SLANT:
                start(block, block, 16 + o, other_r.at[ch, o], across)

    def project(ch, o):
        if "weight" not in once:
            loads[5].wait()
            wx.wait_recv()
            once.add("weight")
        c = cols(ch)
        width = widths[ch]

        @pl.when(middle)
        def _():
            if o == 0:
                arrived(gated.at[q, o, 1 - core, :, c], own_r.at[ch, o])
            else:
                arrived(gated.at[q, o, :, :, c], own_r.at[ch, o])

        arrived(gated.at[1 - q, o, :, :, c], other_r.at[ch, o])
        plane = seq if o == 0 else 1 - seq
        value = None
        for source in range(2):
            left = jnp.concatenate(
                [gated[side, o, source, :, c] for side in range(2)], 1
            )
            right = jnp.concatenate(
                [wb[source, channels(side, plane, starts[ch], width)] for side in range(2)], 0
            )
            term = dot(left, right)
            value = term if value is None else value + term
        if "sum" not in once:
            once.add("sum")
            acc_buf[...] = value
        elif (ch, o) != LAST:
            acc_buf[...] += value
        else:
            fin_buf[...] = (acc_buf[...] + value).astype(BF16).reshape(fin_buf.shape)

    steps = dict(m=more, r=relay, c=compute, g=gates, p=pass_gates, n=gather_near, d=reduce, f=forward, j=project)
    for event in EVENTS:
        steps[event[0]](*[int(a) for a in event[1:]])

    def place(index):
        return out_ref.at[:, pl.ds(pl.multiple_of(index * columns, columns), columns)]

    for k in range(pairs - 1, -1, -1):
        for side in (1 - q, q) if k > 0 else (1 - q,):
            to = 2 * (nearest(p, k, pairs) if k > 0 else p) + side
            start(fin_buf.at[to], place(me), 18, fin_r, {"hist": to})
    keep = pltpu.make_async_copy(fin_buf.at[me], place(me), load_sem.at[6])
    keep.start()
    drained(gb.at[0, 0, 0], 0)
    drained(gb.at[0, 0, 0], 1)
    drained(gb.at[0, 0, 0], 2)
    drained(tb.at[0], 3)
    drained(hb.at[0, 0], 4)
    drained(hb.at[0, 0], 5)
    drained(hb.at[0, 0], 6)

    @pl.when(p > 0)
    def _():
        drained(tb.at[2], 7)

    wx.wait_send()
    drained(send_buf, 9)
    drained(gb.at[0], 19)

    def share(n):
        return pl.ds(0, n * LANES)

    @pl.when(middle)
    def _():
        drained(gb.at[0], 20)
        drained(stage, 11)
        drained(stage, 12)
        drained(stage.at[:, 0], 13)
        drained(stage.at[0, 0], 14)
        if SLANT:
            drained(stage.at[:, 0, :, share(len(SLANT))], 15)

    @pl.when(jnp.logical_not(middle))
    def _():
        if DIRECT:
            drained(send_buf.at[0, :, share(len(DIRECT))], 10)
        for o in range(2):
            rest = len(widths) - sum(unit[1] == o for unit in SLANT)
            if rest:
                drained(gated.at[0, 0, :, :, share(rest)], 16 + o)

    drained(fin_buf.at[:total - 1], 18)
    keep.wait()
    arrived(out_ref.at[:, :(total - 1) * columns], fin_r)


def local_kernel(widths, history, filter_taps, gate_values, out_weight):
    rows, channels = history.shape
    owned = gate_values.shape[0]
    total = lax.axis_size("hist")
    cores = lax.axis_size("chan")
    pairs = total // 2
    tokens = owned * total
    quarter = channels // 4
    columns = out_weight.shape[1]
    part = owned // cores
    forward, inverse = tables(rows, tokens)
    forward = jnp.asarray(forward, F32).astype(BF16)
    inverse = jnp.asarray(inverse, F32).astype(BF16)
    dma = pltpu.SemaphoreType.DMA
    chunks = len(widths)
    each = dma((chunks,))
    scratch = [
        pltpu.VMEM((3, rows, quarter), BF16),
        pltpu.VMEM((2, 2, rows, quarter), BF16),
        pltpu.VMEM((pairs, 2, 2, owned, quarter), BF16),
        pltpu.VMEM((cores,) + out_weight.shape, BF16),
        pltpu.VMEM(forward.shape, BF16),
        pltpu.VMEM(inverse.shape, BF16),
        pltpu.VMEM((chunks, 2 * tokens, 2 * widths[0]), F32),
        pltpu.VMEM((2, tokens, quarter), BF16),
        pltpu.VMEM((2, tokens, quarter), F32),
        pltpu.VMEM((2, tokens, quarter), BF16),
        pltpu.VMEM((2, 2, tokens, quarter), BF16),
        pltpu.VMEM((cores, 2, tokens // cores, quarter), BF16),
        pltpu.VMEM((2, 2, cores, tokens // cores, quarter), BF16),
        pltpu.VMEM((tokens // cores, columns), F32),
        pltpu.VMEM((total, part, columns), BF16),
        dma((7,)), dma((21,)), each, each, each, each, each, dma((3,)), dma((3,)), dma,
        dma((chunks, 2)), dma((chunks, 2)), dma((chunks, 2)), dma((chunks, 2)), dma,
        pltpu.SemaphoreType.REGULAR((pairs - 2,)),
    ]
    return pl.pallas_call(
        functools.partial(kernel, pairs, widths),
        out_shape=jax.ShapeDtypeStruct((part, total * columns), BF16),
        in_specs=[pl.BlockSpec(memory_space=pl.ANY)] * 6,
        out_specs=pl.BlockSpec(memory_space=pl.ANY),
        scratch_shapes=scratch,
        compiler_params=pltpu.CompilerParams(
            collective_id=0, has_side_effects=True, vmem_limit_bytes=67043328
        ),
    )(history, filter_taps, gate_values, out_weight, forward, inverse)


def local(history, filter_taps, gate_values, out_weight):
    rows, channels = history.shape
    owned = gate_values.shape[0]
    total = lax.axis_size("hist")
    cores = lax.axis_size("chan")
    slabs = channels // (4 * LANES)
    fits = (
        total == 8
        and cores == 2
        and lax.axis_size("seq") == 2
        and owned % (16 * cores) == 0
        and rows == owned * total
        and channels % (4 * LANES) == 0
        and slabs == sum(PARTS)
        and out_weight.shape[1] % LANES == 0
    )
    if fits:
        widths = [LANES * part for part in PARTS]
        return local_kernel(widths, history, filter_taps, gate_values, out_weight)
    return local_general(history, filter_taps, gate_values, out_weight)


def solution(mesh):
    return jax.shard_map(
        local,
        mesh=mesh,
        in_specs=(
            P(("seq", "hist"), "chan"),
            P("hist", "chan"),
            P(("seq", "hist"), "chan"),
            P("chan", "hist"),
        ),
        out_specs=P(("seq", "hist", "chan"), None),
        check_vma=False,
    )
```

```python
import functools
import math

import jax
import jax.numpy as jnp
import numpy as np
from jax import lax
from jax.experimental import pallas as pl
from jax.experimental.pallas import tpu as pltpu
from jax.sharding import PartitionSpec as P

MESH = pl.DeviceIdType.MESH
BF16 = jnp.bfloat16
F32 = jnp.float32
LANES = 128
PARTS = (1, 1, 1, 1)
LAST = (3, 1)
DIRECT = ()
SLANT = ((2, 0), (3, 1), (3, 0))
ISSUE = (
    (
        "k", "h", "t0", "t1", "y0", "t2", "t3", "y1", "y2", "y3", "x0",
    ),
    (
        "g", "x1", "d0", "x2", "x3",
    ),
    (
        "d1",
    ),
    (
        "d2",
    ),
    (
        "d3",
    ),
)
EVENTS = (
    "r0", "g", "r1", "c00", "m1", "r2", "c01", "m2", "p", "r3", "n00", "c11", "n01", "c10", "m3",
    "c21", "d00", "n11", "d01", "c20", "n10", "c30", "c31", "n21", "d11", "n20", "d10", "n30", "d21",
    "n31", "d20", "d30", "d31", "f00", "f01", "f11", "f10", "f21", "f20", "f30", "f31", "j00", "j01",
    "j11", "j10", "j21", "j20", "j30", "j31",
)


def tables(local_rows, block_tokens):
    period = local_rows + block_tokens
    modes = period // 2
    odd = 2 * np.arange(modes) + 1
    turn = math.pi / period
    places = np.arange(period)
    phase = (np.outer(odd, places) % (2 * period)) * turn
    forward = np.concatenate([np.cos(phase), np.sin(phase)], 0)
    lags = block_tokens - 1 - np.arange(block_tokens)
    phase = (np.outer(lags, odd) % (2 * period)) * turn
    inverse = np.concatenate([np.cos(phase), -np.sin(phase)], 1) * (2.0 / period)
    return forward, inverse


def spectrum_product(taps, values):
    half = taps.shape[0] // 2
    tc, ts, vc, vs = taps[:half], taps[half:], values[:half], values[half:]
    return tc * vc + ts * vs, tc * vs - ts * vc


def dot(a, b):
    return jnp.dot(a, b, preferred_element_type=F32)


def local_general(history, filter_taps, gate_values, out_weight):
    local_rows, channels = history.shape
    owned_rows = gate_values.shape[0]
    count_hist = lax.axis_size("hist")
    count_chan = lax.axis_size("chan")
    block_tokens = owned_rows * count_hist
    forward, inverse = tables(local_rows, block_tokens)
    forward = jnp.asarray(forward, F32)
    forward_high = forward.astype(BF16)
    forward_low = (forward - forward_high.astype(F32)).astype(BF16)
    inverse = jnp.asarray(inverse, F32)
    next_taps = lax.ppermute(
        filter_taps, "hist", [(source, source - 1) for source in range(1, count_hist)]
    )
    extended = jnp.concatenate([filter_taps, next_taps], 0)[: forward.shape[1]]
    spec_taps = dot(forward_high, extended) + dot(forward_low, extended)
    spec_input = dot(forward_high[:, :local_rows], history) + dot(
        forward_low[:, :local_rows], history
    )
    spectrum = jnp.concatenate(spectrum_product(spec_taps, spec_input), 0)
    partial_conv = jnp.dot(
        inverse, spectrum, precision=lax.Precision.HIGHEST, preferred_element_type=F32
    )
    conv = lax.psum_scatter(partial_conv, "hist", scatter_dimension=0, tiled=True)
    gated = (conv * gate_values.astype(F32)).astype(BF16)
    partial_value = dot(lax.all_gather(gated, "hist", axis=0, tiled=True), out_weight)
    columns = partial_value.shape[1]
    half_rows = owned_rows // count_chan
    ordered = partial_value.reshape(count_hist, count_chan, half_rows, columns)
    ordered = ordered.transpose(1, 0, 2, 3).reshape(-1, columns)
    summed = lax.psum_scatter(ordered.astype(BF16), "chan", scatter_dimension=0, tiled=True)
    return lax.all_to_all(summed, "hist", split_axis=0, concat_axis=1, tiled=True)


def nearest(p, k, pairs):
    low = jnp.minimum(p, pairs - 1 - p)
    spot = jnp.where(k <= 2 * low, jnp.where(k % 2 == 1, low - (k + 1) // 2, low + k // 2), k)
    return jnp.where(p * 2 < pairs, spot, pairs - 1 - spot)


def kernel(
    pairs, widths, hist_ref, taps_ref, gate_ref, weight_ref, fwd_ref, inv_ref, out_ref,
    tb, hb, gb, wb, fb, ib, spec_buf, send_buf, own_buf, near_buf, far_buf, stage, gated, acc_buf,
    fin_buf, load_sem, sent, ty_r, hy_r, hx_r, hd_r, zt_r, gate_r, gz_r, wx_r, near_r, far_r, own_r,
    other_r, fin_r, ready_sem,
):
    me = lax.axis_index("hist")
    core = lax.axis_index("chan")
    seq = lax.axis_index("seq")
    p = me // 2
    q = me % 2
    total = 2 * pairs
    rows = hist_ref.shape[0]
    quarter = hist_ref.shape[1] // 4
    half = 2 * quarter
    columns = weight_ref.shape[1]
    partner = 2 * p + (1 - q)
    modes = fb.shape[0] // 2
    across = {"hist": partner}
    beyond = {"seq": 1 - seq}
    diagonal = {"hist": partner, "seq": 1 - seq}
    below = {"hist": jnp.maximum(me - 2, 0)}
    starts = [sum(widths[:i]) for i in range(len(widths) + 1)]
    chunks = range(len(widths))
    middle = (p > 0) & (p < pairs - 1)
    inner = jnp.where(p < 2, 1, 2)
    outer = jnp.where(p < 2, 0, 3)
    to_inner = {"hist": 2 * inner + q}
    to_facing = {"hist": 2 * (3 - inner) + q}

    def remote(src, dst, send, recv, where):
        return pltpu.make_async_remote_copy(
            src_ref=src, dst_ref=dst, send_sem=send, recv_sem=recv,
            device_id=where, device_id_type=MESH,
        )

    def start(src, dst, send, recv, where):
        remote(src, dst, sent.at[send], recv, where).start()

    def arrived(dst, recv):
        remote(dst, dst, load_sem.at[0], recv, {"chan": 1 - core}).wait_recv()

    def drained(src, send):
        remote(src, src, sent.at[send], load_sem.at[0], {"chan": 1 - core}).wait_send()

    def greet(sem, where):
        pl.semaphore_signal(sem, inc=1, device_id=where, device_id_type=MESH)

    def greet_line(sem):
        @pl.when(p > 0)
        def _():
            greet(sem, {"hist": me - 2})

        @pl.when(p < pairs - 1)
        def _():
            greet(sem, {"hist": me + 2})

    barrier = pltpu.get_barrier_semaphore()
    beside = jnp.minimum(p, 1) + jnp.minimum(pairs - 1 - p, 1)
    greet(barrier, across)
    greet_line(barrier)
    greet(barrier, beyond)
    greet(barrier, {"chan": 1 - core})

    def channels(y, x, at=0, width=quarter):
        return pl.ds(pl.multiple_of(y * half + x * quarter + at, LANES), width)

    mine = channels(q, seq)
    loads = [
        pltpu.make_async_copy(taps_ref.at[:, mine], tb.at[q], load_sem.at[0]),
        pltpu.make_async_copy(hist_ref.at[:, mine], hb.at[q, 0], load_sem.at[1]),
        pltpu.make_async_copy(fwd_ref, fb, load_sem.at[2]),
        pltpu.make_async_copy(inv_ref, ib, load_sem.at[3]),
        pltpu.make_async_copy(gate_ref.at[:, mine], gb.at[p, q, 0], load_sem.at[4]),
        pltpu.make_async_copy(weight_ref, wb.at[core], load_sem.at[5]),
    ]
    for copy in loads:
        copy.start()

    @pl.when(p == pairs - 1)
    def _():
        tb[2] = jnp.zeros(tb.shape[1:], BF16)

    pl.semaphore_wait(barrier, 3 + beside)

    def cols(ch):
        return pl.ds(starts[ch], widths[ch])

    def from_hbm(ref, y, x, ch):
        return ref.at[:, channels(y, x, starts[ch], widths[ch])]

    def issue(entry):
        kind = entry[0]
        if kind == "k":
            start(gate_ref.at[:, channels(q, 1 - seq)], gb.at[p, q, 1], 0, gate_r.at[0], beyond)
            return
        if kind == "g":
            start(gate_ref.at[:, channels(1 - q, 1 - seq)], gb.at[p, q, 1], 1, gate_r.at[1], diagonal)
            return
        if kind == "h":
            start(gate_ref.at[:, channels(1 - q, seq)], gb.at[p, q, 0], 2, gate_r.at[2], across)
            return
        ch = int(entry[1:])
        c = cols(ch)
        if kind == "t":
            start(from_hbm(taps_ref, 1 - q, seq, ch), tb.at[q, :, c], 3, ty_r.at[ch], across)
        if kind == "y":
            start(from_hbm(hist_ref, 1 - q, seq, ch), hb.at[q, 0, :, c], 4, hy_r.at[ch], across)
        if kind == "x":
            start(from_hbm(hist_ref, q, 1 - seq, ch), hb.at[q, 1, :, c], 5, hx_r.at[ch], beyond)
        if kind == "d":
            start(from_hbm(hist_ref, 1 - q, 1 - seq, ch), hb.at[q, 1, :, c], 6, hd_r.at[ch], diagonal)

    for entry in ISSUE[0]:
        issue(entry)
    for ch in chunks:
        @pl.when((q == 0) & (p > 0))
        def _():
            start(from_hbm(taps_ref, 0, seq, ch), tb.at[2, :, cols(ch)], 7, zt_r.at[ch], below)

    for r in range(pairs - 2):
        greet_line(ready_sem.at[r])
        if r == 0:
            greet(ready_sem.at[r], across)
            pl.semaphore_wait(ready_sem.at[r], beside + 1)
            for entry in ISSUE[1]:
                issue(entry)
        else:
            pl.semaphore_wait(ready_sem.at[r], beside)
    wx = remote(weight_ref, wb.at[core], sent.at[8], wx_r, {"chan": 1 - core})
    wx.start()

    def more(i):
        for entry in ISSUE[i + 1]:
            issue(entry)

    def relay(ch):
        c = cols(ch)

        @pl.when(q == 1)
        def _():
            arrived(tb.at[1 - q, :, c], ty_r.at[ch])

        @pl.when((q == 1) & (p > 0))
        def _():
            start(tb.at[0, :, c], tb.at[2, :, c], 7, zt_r.at[ch], below)

    once = set()

    def compute(ch, o):
        if "load" not in once:
            for copy in loads[:4]:
                copy.wait()
            once.add("load")
        c = cols(ch)
        width = widths[ch]
        first, second = fb[:, :rows], fb[:, rows:]
        if ("taps", ch) not in once:
            once.add(("taps", ch))

            @pl.when(q == 0)
            def _():
                arrived(tb.at[1 - q, :, c], ty_r.at[ch])

            @pl.when(p < pairs - 1)
            def _():
                arrived(tb.at[2, :, c], zt_r.at[ch])

            t1 = tb[1, :, c]
            spec_buf[ch] = dot(first, jnp.concatenate([tb[0, :, c], t1], 1)) + dot(
                second, jnp.concatenate([t1, tb[2, :, c]], 1)
            )
        if o == 0:
            arrived(hb.at[1 - q, 0, :, c], hy_r.at[ch])
        else:
            arrived(hb.at[q, 1, :, c], hx_r.at[ch])
            arrived(hb.at[1 - q, 1, :, c], hd_r.at[ch])
        values = dot(first, jnp.concatenate([hb[0, o, :, c], hb[1, o, :, c]], 1))
        real, imag = spectrum_product(spec_buf[ch], values)
        real = (real[:, :width] + real[:, width:]).astype(BF16)
        imag = (imag[:, :width] + imag[:, width:]).astype(BF16)
        conv = dot(ib[:, :modes], real) + dot(ib[:, modes:], imag)
        direct = (ch, o) in DIRECT
        if direct:
            send_buf[o, :, c] = conv.astype(BF16)
            own_buf[o, :, c] = conv

            @pl.when(middle)
            def _():
                start(send_buf.at[o, :, c], far_buf.at[0, o, :, c], 9, far_r.at[ch, o], to_facing)

            @pl.when(jnp.logical_not(middle))
            def _():
                start(send_buf.at[o, :, c], far_buf.at[1, o, :, c], 10, far_r.at[ch, o], to_facing)
                start(send_buf.at[o, :, c], near_buf.at[o, :, c], 9, near_r.at[ch, o], to_inner)
        else:
            @pl.when(middle)
            def _():
                own_buf[o, :, c] = conv

            @pl.when(jnp.logical_not(middle))
            def _():
                send_buf[o, :, c] = conv.astype(BF16)
                start(send_buf.at[o, :, c], near_buf.at[o, :, c], 9, near_r.at[ch, o], to_inner)

    def gates():
        loads[4].wait()
        arrived(gb.at[p, 1 - q, 0], gate_r.at[2])
        arrived(gb.at[p, q, 1], gate_r.at[0])
        arrived(gb.at[p, 1 - q, 1], gate_r.at[1])

        @pl.when(middle)
        def _():
            start(gb.at[p], gb.at[p], 19, gz_r.at[1], to_facing)

        @pl.when(jnp.logical_not(middle))
        def _():
            start(gb.at[p], gb.at[p], 19, gz_r.at[0], to_inner)

    def pass_gates():
        @pl.when(middle)
        def _():
            arrived(gb.at[outer], gz_r.at[0])
            start(gb.at[outer], gb.at[outer], 20, gz_r.at[2], to_facing)

    def gather_near(ch, o):
        c = cols(ch)

        @pl.when(middle)
        def _():
            arrived(near_buf.at[o, :, c], near_r.at[ch, o])
            value = own_buf[o, :, c] + near_buf[o, :, c].astype(F32)
            own_buf[o, :, c] = value
            if (ch, o) not in DIRECT:
                send_buf[o, :, c] = value.astype(BF16)
                start(send_buf.at[o, :, c], far_buf.at[0, o, :, c], 9, far_r.at[ch, o], to_facing)

    def reduce(ch, o):
        c = cols(ch)
        width = widths[ch]
        first_time = "gates" not in once
        once.add("gates")

        @pl.when(middle)
        def _():
            if first_time:
                arrived(gb.at[3 - inner], gz_r.at[1])
                arrived(gb.at[3 - outer], gz_r.at[2])
            if (ch, o) in DIRECT:
                arrived(far_buf.at[:, o, :, c], far_r.at[ch, o])
                value = own_buf[o, :, c] + far_buf[0, o, :, c].astype(F32)
                value = value + far_buf[1, o, :, c].astype(F32)
            else:
                arrived(far_buf.at[0, o, :, c], far_r.at[ch, o])
                value = own_buf[o, :, c] + far_buf[0, o, :, c].astype(F32)
            gate = gb[:, :, o, :, c].astype(F32).reshape(value.shape)
            block = (value * gate).astype(BF16).reshape(total, 2, -1, width)
            for kappa in range(2):
                stage[kappa, o, :, c] = block[:, kappa].reshape(-1, width)
            there = gated.at[q, o, core, :, c]
            plane = seq if o == 0 else 1 - seq
            for kappa in range(2):
                start(stage.at[kappa, o, :, c], there, 11, own_r.at[ch, o],
                      {"hist": 2 * outer + q, "seq": plane, "chan": kappa})
            if (ch, o) in SLANT:
                for kappa in range(2):
                    start(stage.at[kappa, o, :, c], there, 15, other_r.at[ch, o],
                          {"hist": 2 * outer + 1 - q, "seq": plane, "chan": kappa})
            for kappa in range(2):
                start(stage.at[kappa, o, :, c], there, 12, other_r.at[ch, o],
                      {"hist": partner, "seq": plane, "chan": kappa})
            if o == 1:
                for kappa in range(2):
                    start(stage.at[kappa, o, :, c], there, 13, own_r.at[ch, o],
                          {"seq": plane, "chan": kappa})
            else:
                start(stage.at[1 - core, o, :, c], there, 14, own_r.at[ch, o], {"chan": 1 - core})
                gated[q, o, core, :, c] = stage[core, o, :, c]

    def forward(ch, o):
        c = cols(ch)
        block = gated.at[q, o, :, :, c]

        @pl.when(jnp.logical_not(middle))
        def _():
            arrived(block, own_r.at[ch, o])
            if (ch, o) not in SLANT:
                start(block, block, 16 + o, other_r.at[ch, o], across)

    def project(ch, o):
        if "weight" not in once:
            loads[5].wait()
            wx.wait_recv()
            once.add("weight")
        c = cols(ch)
        width = widths[ch]

        @pl.when(middle)
        def _():
            if o == 0:
                arrived(gated.at[q, o, 1 - core, :, c], own_r.at[ch, o])
            else:
                arrived(gated.at[q, o, :, :, c], own_r.at[ch, o])

        arrived(gated.at[1 - q, o, :, :, c], other_r.at[ch, o])
        plane = seq if o == 0 else 1 - seq
        value = None
        for source in range(2):
            left = jnp.concatenate(
                [gated[side, o, source, :, c] for side in range(2)], 1
            )
            right = jnp.concatenate(
                [wb[source, channels(side, plane, starts[ch], width)] for side in range(2)], 0
            )
            term = dot(left, right)
            value = term if value is None else value + term
        if "sum" not in once:
            once.add("sum")
            acc_buf[...] = value
        elif (ch, o) != LAST:
            acc_buf[...] += value
        else:
            fin_buf[...] = (acc_buf[...] + value).astype(BF16).reshape(fin_buf.shape)

    steps = dict(m=more, r=relay, c=compute, g=gates, p=pass_gates, n=gather_near, d=reduce, f=forward, j=project)
    for event in EVENTS:
        steps[event[0]](*[int(a) for a in event[1:]])

    def place(index):
        return out_ref.at[:, pl.ds(pl.multiple_of(index * columns, columns), columns)]

    for k in range(pairs - 1, -1, -1):
        for side in (1 - q, q) if k > 0 else (1 - q,):
            to = 2 * (nearest(p, k, pairs) if k > 0 else p) + side
            start(fin_buf.at[to], place(me), 18, fin_r, {"hist": to})
    keep = pltpu.make_async_copy(fin_buf.at[me], place(me), load_sem.at[6])
    keep.start()
    drained(gb.at[0, 0, 0], 0)
    drained(gb.at[0, 0, 0], 1)
    drained(gb.at[0, 0, 0], 2)
    drained(tb.at[0], 3)
    drained(hb.at[0, 0], 4)
    drained(hb.at[0, 0], 5)
    drained(hb.at[0, 0], 6)

    @pl.when(p > 0)
    def _():
        drained(tb.at[2], 7)

    wx.wait_send()
    drained(send_buf, 9)
    drained(gb.at[0], 19)

    def share(n):
        return pl.ds(0, n * LANES)

    @pl.when(middle)
    def _():
        drained(gb.at[0], 20)
        drained(stage, 11)
        drained(stage, 12)
        drained(stage.at[:, 0], 13)
        drained(stage.at[0, 0], 14)
        if SLANT:
            drained(stage.at[:, 0, :, share(len(SLANT))], 15)

    @pl.when(jnp.logical_not(middle))
    def _():
        if DIRECT:
            drained(send_buf.at[0, :, share(len(DIRECT))], 10)
        for o in range(2):
            rest = len(widths) - sum(unit[1] == o for unit in SLANT)
            if rest:
                drained(gated.at[0, 0, :, :, share(rest)], 16 + o)

    drained(fin_buf.at[:total - 1], 18)
    keep.wait()
    arrived(out_ref.at[:, :(total - 1) * columns], fin_r)


def local_kernel(widths, history, filter_taps, gate_values, out_weight):
    rows, channels = history.shape
    owned = gate_values.shape[0]
    total = lax.axis_size("hist")
    cores = lax.axis_size("chan")
    pairs = total // 2
    tokens = owned * total
    quarter = channels // 4
    columns = out_weight.shape[1]
    part = owned // cores
    forward, inverse = tables(rows, tokens)
    forward = jnp.asarray(forward, F32).astype(BF16)
    inverse = jnp.asarray(inverse, F32).astype(BF16)
    dma = pltpu.SemaphoreType.DMA
    chunks = len(widths)
    each = dma((chunks,))
    scratch = [
        pltpu.VMEM((3, rows, quarter), BF16),
        pltpu.VMEM((2, 2, rows, quarter), BF16),
        pltpu.VMEM((pairs, 2, 2, owned, quarter), BF16),
        pltpu.VMEM((cores,) + out_weight.shape, BF16),
        pltpu.VMEM(forward.shape, BF16),
        pltpu.VMEM(inverse.shape, BF16),
        pltpu.VMEM((chunks, 2 * tokens, 2 * widths[0]), F32),
        pltpu.VMEM((2, tokens, quarter), BF16),
        pltpu.VMEM((2, tokens, quarter), F32),
        pltpu.VMEM((2, tokens, quarter), BF16),
        pltpu.VMEM((2, 2, tokens, quarter), BF16),
        pltpu.VMEM((cores, 2, tokens // cores, quarter), BF16),
        pltpu.VMEM((2, 2, cores, tokens // cores, quarter), BF16),
        pltpu.VMEM((tokens // cores, columns), F32),
        pltpu.VMEM((total, part, columns), BF16),
        dma((7,)), dma((21,)), each, each, each, each, each, dma((3,)), dma((3,)), dma,
        dma((chunks, 2)), dma((chunks, 2)), dma((chunks, 2)), dma((chunks, 2)), dma,
        pltpu.SemaphoreType.REGULAR((pairs - 2,)),
    ]
    return pl.pallas_call(
        functools.partial(kernel, pairs, widths),
        out_shape=jax.ShapeDtypeStruct((part, total * columns), BF16),
        in_specs=[pl.BlockSpec(memory_space=pl.ANY)] * 6,
        out_specs=pl.BlockSpec(memory_space=pl.ANY),
        scratch_shapes=scratch,
        compiler_params=pltpu.CompilerParams(
            collective_id=0, has_side_effects=True, vmem_limit_bytes=25165824
        ),
    )(*[pltpu.with_memory_space_constraint(x, pltpu.HBM) for x in (history, filter_taps, gate_values, out_weight, forward, inverse)])


def local(history, filter_taps, gate_values, out_weight):
    rows, channels = history.shape
    owned = gate_values.shape[0]
    total = lax.axis_size("hist")
    cores = lax.axis_size("chan")
    slabs = channels // (4 * LANES)
    fits = (
        total == 8
        and cores == 2
        and lax.axis_size("seq") == 2
        and owned % (16 * cores) == 0
        and rows == owned * total
        and channels % (4 * LANES) == 0
        and slabs == sum(PARTS)
        and out_weight.shape[1] % LANES == 0
    )
    if fits:
        widths = [LANES * part for part in PARTS]
        return local_kernel(widths, history, filter_taps, gate_values, out_weight)
    return local_general(history, filter_taps, gate_values, out_weight)


def solution(mesh):
    return jax.shard_map(
        local,
        mesh=mesh,
        in_specs=(
            P(("seq", "hist"), "chan"),
            P("hist", "chan"),
            P(("seq", "hist"), "chan"),
            P("chan", "hist"),
        ),
        out_specs=P(("seq", "hist", "chan"), None),
        check_vma=False,
    )
```

```python
import functools
import math

import jax
import jax.numpy as jnp
import numpy as np
from jax import lax
from jax.experimental import pallas as pl
from jax.experimental.pallas import tpu as pltpu
from jax.sharding import PartitionSpec as P

MESH = pl.DeviceIdType.MESH
BF16 = jnp.bfloat16
F32 = jnp.float32
LANES = 128
PARTS = (1, 1, 1, 1)
LAST = (3, 1)
DIRECT = ()
SLANT = ((2, 0), (3, 1), (3, 0))
ISSUE = (
    (
        "k", "h", "t0", "t1", "y0", "t2", "t3", "y1", "y2", "y3", "x0",
    ),
    (
        "g", "x1", "d0", "x2", "x3",
    ),
    (
        "d1",
    ),
    (
        "d2",
    ),
    (
        "d3",
    ),
)
EVENTS = (
    "r0", "g", "r1", "c00", "m1", "r2", "c01", "m2", "p", "r3", "n00", "c11", "n01", "c10", "m3",
    "c21", "d00", "n11", "d01", "c20", "n10", "c30", "c31", "n21", "d11", "n20", "d10", "n30", "d21",
    "n31", "d20", "d30", "d31", "f00", "f01", "f11", "f10", "f21", "f20", "f30", "f31", "j00", "j01",
    "j11", "j10", "j21", "j20", "j30", "j31",
)


def tables(local_rows, block_tokens):
    period = local_rows + block_tokens
    modes = period // 2
    odd = 2 * np.arange(modes) + 1
    turn = math.pi / period
    places = np.arange(period)
    phase = (np.outer(odd, places) % (2 * period)) * turn
    forward = np.concatenate([np.cos(phase), np.sin(phase)], 0)
    lags = block_tokens - 1 - np.arange(block_tokens)
    phase = (np.outer(lags, odd) % (2 * period)) * turn
    inverse = np.concatenate([np.cos(phase), -np.sin(phase)], 1) * (2.0 / period)
    return forward, inverse


def spectrum_product(taps, values):
    half = taps.shape[0] // 2
    tc, ts, vc, vs = taps[:half], taps[half:], values[:half], values[half:]
    return tc * vc + ts * vs, tc * vs - ts * vc


def dot(a, b):
    return jnp.dot(a, b, preferred_element_type=F32)


def local_general(history, filter_taps, gate_values, out_weight):
    local_rows, channels = history.shape
    owned_rows = gate_values.shape[0]
    count_hist = lax.axis_size("hist")
    count_chan = lax.axis_size("chan")
    block_tokens = owned_rows * count_hist
    forward, inverse = tables(local_rows, block_tokens)
    forward = jnp.asarray(forward, F32)
    forward_high = forward.astype(BF16)
    forward_low = (forward - forward_high.astype(F32)).astype(BF16)
    inverse = jnp.asarray(inverse, F32)
    next_taps = lax.ppermute(
        filter_taps, "hist", [(source, source - 1) for source in range(1, count_hist)]
    )
    extended = jnp.concatenate([filter_taps, next_taps], 0)[: forward.shape[1]]
    spec_taps = dot(forward_high, extended) + dot(forward_low, extended)
    spec_input = dot(forward_high[:, :local_rows], history) + dot(
        forward_low[:, :local_rows], history
    )
    spectrum = jnp.concatenate(spectrum_product(spec_taps, spec_input), 0)
    partial_conv = jnp.dot(
        inverse, spectrum, precision=lax.Precision.HIGHEST, preferred_element_type=F32
    )
    conv = lax.psum_scatter(partial_conv, "hist", scatter_dimension=0, tiled=True)
    gated = (conv * gate_values.astype(F32)).astype(BF16)
    partial_value = dot(lax.all_gather(gated, "hist", axis=0, tiled=True), out_weight)
    columns = partial_value.shape[1]
    half_rows = owned_rows // count_chan
    ordered = partial_value.reshape(count_hist, count_chan, half_rows, columns)
    ordered = ordered.transpose(1, 0, 2, 3).reshape(-1, columns)
    summed = lax.psum_scatter(ordered.astype(BF16), "chan", scatter_dimension=0, tiled=True)
    return lax.all_to_all(summed, "hist", split_axis=0, concat_axis=1, tiled=True)


def nearest(p, k, pairs):
    low = jnp.minimum(p, pairs - 1 - p)
    spot = jnp.where(k <= 2 * low, jnp.where(k % 2 == 1, low - (k + 1) // 2, low + k // 2), k)
    return jnp.where(p * 2 < pairs, spot, pairs - 1 - spot)


def kernel(
    pairs, widths, hist_ref, taps_ref, gate_ref, weight_ref, fwd_ref, inv_ref, out_ref,
    tb, hb, gb, wb, fb, ib, spec_buf, send_buf, own_buf, near_buf, far_buf, stage, gated, acc_buf,
    fin_buf, load_sem, sent, ty_r, hy_r, hx_r, zt_r, gate_r, gz_r, wx_r, near_r, far_r, own_r,
    other_r, fin_r, ready_sem,
):
    me = lax.axis_index("hist")
    core = lax.axis_index("chan")
    seq = lax.axis_index("seq")
    p = me // 2
    q = me % 2
    total = 2 * pairs
    rows = hist_ref.shape[0]
    quarter = hist_ref.shape[1] // 4
    half = 2 * quarter
    columns = weight_ref.shape[1]
    partner = 2 * p + (1 - q)
    modes = fb.shape[0] // 2
    across = {"hist": partner}
    beyond = {"seq": 1 - seq}
    diagonal = {"hist": partner, "seq": 1 - seq}
    below = {"hist": jnp.maximum(me - 2, 0)}
    starts = [sum(widths[:i]) for i in range(len(widths) + 1)]
    chunks = range(len(widths))
    middle = (p > 0) & (p < pairs - 1)
    inner = jnp.where(p < 2, 1, 2)
    outer = jnp.where(p < 2, 0, 3)
    to_inner = {"hist": 2 * inner + q}
    to_facing = {"hist": 2 * (3 - inner) + q}

    def remote(src, dst, send, recv, where):
        return pltpu.make_async_remote_copy(
            src_ref=src, dst_ref=dst, send_sem=send, recv_sem=recv,
            device_id=where, device_id_type=MESH,
        )

    def start(src, dst, send, recv, where):
        remote(src, dst, sent.at[send], recv, where).start()

    def arrived(dst, recv):
        remote(dst, dst, load_sem.at[0], recv, {"chan": 1 - core}).wait_recv()

    def drained(src, send):
        remote(src, src, sent.at[send], load_sem.at[0], {"chan": 1 - core}).wait_send()

    def greet(sem, where):
        pl.semaphore_signal(sem, inc=1, device_id=where, device_id_type=MESH)

    def greet_line(sem):
        @pl.when(p > 0)
        def _():
            greet(sem, {"hist": me - 2})

        @pl.when(p < pairs - 1)
        def _():
            greet(sem, {"hist": me + 2})

    barrier = pltpu.get_barrier_semaphore()
    beside = jnp.minimum(p, 1) + jnp.minimum(pairs - 1 - p, 1)
    greet(barrier, across)
    greet_line(barrier)
    greet(barrier, beyond)
    greet(barrier, {"chan": 1 - core})

    def channels(y, x, at=0, width=quarter):
        return pl.ds(pl.multiple_of(y * half + x * quarter + at, LANES), width)

    mine = channels(q, seq)
    loads = [
        pltpu.make_async_copy(taps_ref.at[:, mine], tb.at[q], load_sem.at[0]),
        pltpu.make_async_copy(hist_ref.at[:, mine], hb.at[q, 0], load_sem.at[1]),
        pltpu.make_async_copy(fwd_ref, fb, load_sem.at[2]),
        pltpu.make_async_copy(inv_ref, ib, load_sem.at[3]),
        pltpu.make_async_copy(gate_ref.at[:, mine], gb.at[p, q, 0], load_sem.at[4]),
        pltpu.make_async_copy(weight_ref, wb.at[core], load_sem.at[5]),
    ]
    for copy in loads:
        copy.start()

    @pl.when(p == pairs - 1)
    def _():
        tb[2] = jnp.zeros(tb.shape[1:], BF16)

    pl.semaphore_wait(barrier, 3 + beside)

    def cols(ch):
        return pl.ds(starts[ch], widths[ch])

    def from_hbm(ref, y, x, ch):
        return ref.at[:, channels(y, x, starts[ch], widths[ch])]

    def issue(entry):
        kind = entry[0]
        if kind == "k":
            start(gate_ref.at[:, channels(q, 1 - seq)], gb.at[p, q, 1], 0, gate_r, beyond)
            return
        if kind == "g":
            start(gate_ref.at[:, channels(1 - q, 1 - seq)], gb.at[p, q, 1], 0, gate_r, diagonal)
            return
        if kind == "h":
            start(gate_ref.at[:, channels(1 - q, seq)], gb.at[p, q, 0], 0, gate_r, across)
            return
        ch = int(entry[1:])
        c = cols(ch)
        if kind == "t":
            start(from_hbm(taps_ref, 1 - q, seq, ch), tb.at[q, :, c], 3, ty_r.at[ch], across)
        if kind == "y":
            start(from_hbm(hist_ref, 1 - q, seq, ch), hb.at[q, 0, :, c], 3, hy_r.at[ch], across)
        if kind == "x":
            start(from_hbm(hist_ref, q, 1 - seq, ch), hb.at[q, 1, :, c], 3, hx_r.at[ch], beyond)
        if kind == "d":
            start(from_hbm(hist_ref, 1 - q, 1 - seq, ch), hb.at[q, 1, :, c], 3, hx_r.at[ch], diagonal)

    for entry in ISSUE[0]:
        issue(entry)
    for ch in chunks:
        @pl.when((q == 0) & (p > 0))
        def _():
            start(from_hbm(taps_ref, 0, seq, ch), tb.at[2, :, cols(ch)], 7, zt_r.at[ch], below)

    for r in range(pairs - 2):
        greet_line(ready_sem.at[r])
        if r == 0:
            greet(ready_sem.at[r], across)
            pl.semaphore_wait(ready_sem.at[r], beside + 1)
            for entry in ISSUE[1]:
                issue(entry)
        else:
            pl.semaphore_wait(ready_sem.at[r], beside)
    wx = remote(weight_ref, wb.at[core], sent.at[8], wx_r, {"chan": 1 - core})
    wx.start()

    def more(i):
        for entry in ISSUE[i + 1]:
            issue(entry)

    def relay(ch):
        c = cols(ch)

        @pl.when(q == 1)
        def _():
            arrived(tb.at[1 - q, :, c], ty_r.at[ch])

        @pl.when((q == 1) & (p > 0))
        def _():
            start(tb.at[0, :, c], tb.at[2, :, c], 7, zt_r.at[ch], below)

    once = set()

    def compute(ch, o):
        if "load" not in once:
            for copy in loads[:4]:
                copy.wait()
            once.add("load")
        c = cols(ch)
        width = widths[ch]
        first, second = fb[:, :rows], fb[:, rows:]
        if ("taps", ch) not in once:
            once.add(("taps", ch))

            @pl.when(q == 0)
            def _():
                arrived(tb.at[1 - q, :, c], ty_r.at[ch])

            @pl.when(p < pairs - 1)
            def _():
                arrived(tb.at[2, :, c], zt_r.at[ch])

            t1 = tb[1, :, c]
            spec_buf[ch] = dot(first, jnp.concatenate([tb[0, :, c], t1], 1)) + dot(
                second, jnp.concatenate([t1, tb[2, :, c]], 1)
            )
        if o == 0:
            arrived(hb.at[1 - q, 0, :, c], hy_r.at[ch])
        else:
            arrived(hb.at[:, 1, :, c], hx_r.at[ch])
        values = dot(first, jnp.concatenate([hb[0, o, :, c], hb[1, o, :, c]], 1))
        real, imag = spectrum_product(spec_buf[ch], values)
        real = (real[:, :width] + real[:, width:]).astype(BF16)
        imag = (imag[:, :width] + imag[:, width:]).astype(BF16)
        conv = dot(ib[:, :modes], real) + dot(ib[:, modes:], imag)
        direct = (ch, o) in DIRECT
        if direct:
            send_buf[o, :, c] = conv.astype(BF16)
            own_buf[o, :, c] = conv

            @pl.when(middle)
            def _():
                start(send_buf.at[o, :, c], far_buf.at[0, o, :, c], 9, far_r.at[ch, o], to_facing)

            @pl.when(jnp.logical_not(middle))
            def _():
                start(send_buf.at[o, :, c], far_buf.at[1, o, :, c], 10, far_r.at[ch, o], to_facing)
                start(send_buf.at[o, :, c], near_buf.at[o, :, c], 9, near_r.at[ch, o], to_inner)
        else:
            @pl.when(middle)
            def _():
                own_buf[o, :, c] = conv

            @pl.when(jnp.logical_not(middle))
            def _():
                send_buf[o, :, c] = conv.astype(BF16)
                start(send_buf.at[o, :, c], near_buf.at[o, :, c], 9, near_r.at[ch, o], to_inner)

    def gates():
        loads[4].wait()
        arrived(gb.at[:3, 0, 0], gate_r)

        @pl.when(middle)
        def _():
            start(gb.at[p], gb.at[p], 5, gz_r.at[1], to_facing)

        @pl.when(jnp.logical_not(middle))
        def _():
            start(gb.at[p], gb.at[p], 5, gz_r.at[0], to_inner)

    def pass_gates():
        @pl.when(middle)
        def _():
            arrived(gb.at[outer], gz_r.at[0])
            start(gb.at[outer], gb.at[outer], 6, gz_r.at[2], to_facing)

    def gather_near(ch, o):
        c = cols(ch)

        @pl.when(middle)
        def _():
            arrived(near_buf.at[o, :, c], near_r.at[ch, o])
            value = own_buf[o, :, c] + near_buf[o, :, c].astype(F32)
            own_buf[o, :, c] = value
            if (ch, o) not in DIRECT:
                send_buf[o, :, c] = value.astype(BF16)
                start(send_buf.at[o, :, c], far_buf.at[0, o, :, c], 9, far_r.at[ch, o], to_facing)

    def reduce(ch, o):
        c = cols(ch)
        width = widths[ch]
        first_time = "gates" not in once
        once.add("gates")

        @pl.when(middle)
        def _():
            if first_time:
                arrived(gb.at[3 - inner], gz_r.at[1])
                arrived(gb.at[3 - outer], gz_r.at[2])
            if (ch, o) in DIRECT:
                arrived(far_buf.at[:, o, :, c], far_r.at[ch, o])
                value = own_buf[o, :, c] + far_buf[0, o, :, c].astype(F32)
                value = value + far_buf[1, o, :, c].astype(F32)
            else:
                arrived(far_buf.at[0, o, :, c], far_r.at[ch, o])
                value = own_buf[o, :, c] + far_buf[0, o, :, c].astype(F32)
            gate = gb[:, :, o, :, c].astype(F32).reshape(value.shape)
            block = (value * gate).astype(BF16).reshape(total, 2, -1, width)
            for kappa in range(2):
                stage[kappa, o, :, c] = block[:, kappa].reshape(-1, width)
            there = gated.at[q, o, core, :, c]
            plane = seq if o == 0 else 1 - seq
            for kappa in range(2):
                start(stage.at[kappa, o, :, c], there, 11, own_r.at[ch, o],
                      {"hist": 2 * outer + q, "seq": plane, "chan": kappa})
            if (ch, o) in SLANT:
                for kappa in range(2):
                    start(stage.at[kappa, o, :, c], there, 15, other_r.at[ch, o],
                          {"hist": 2 * outer + 1 - q, "seq": plane, "chan": kappa})
            for kappa in range(2):
                start(stage.at[kappa, o, :, c], there, 12, other_r.at[ch, o],
                      {"hist": partner, "seq": plane, "chan": kappa})
            if o == 1:
                for kappa in range(2):
                    start(stage.at[kappa, o, :, c], there, 13, own_r.at[ch, o],
                          {"seq": plane, "chan": kappa})
            else:
                start(stage.at[1 - core, o, :, c], there, 14, own_r.at[ch, o], {"chan": 1 - core})
                gated[q, o, core, :, c] = stage[core, o, :, c]

    def forward(ch, o):
        c = cols(ch)
        block = gated.at[q, o, :, :, c]

        @pl.when(jnp.logical_not(middle))
        def _():
            arrived(block, own_r.at[ch, o])
            if (ch, o) not in SLANT:
                start(block, block, 1 + o, other_r.at[ch, o], across)

    def project(ch, o):
        if "weight" not in once:
            loads[5].wait()
            wx.wait_recv()
            once.add("weight")
        c = cols(ch)
        width = widths[ch]

        @pl.when(middle)
        def _():
            if o == 0:
                arrived(gated.at[q, o, 1 - core, :, c], own_r.at[ch, o])
            else:
                arrived(gated.at[q, o, :, :, c], own_r.at[ch, o])

        arrived(gated.at[1 - q, o, :, :, c], other_r.at[ch, o])
        plane = seq if o == 0 else 1 - seq
        value = None
        for source in range(2):
            left = jnp.concatenate(
                [gated[side, o, source, :, c] for side in range(2)], 1
            )
            right = jnp.concatenate(
                [wb[source, channels(side, plane, starts[ch], width)] for side in range(2)], 0
            )
            term = dot(left, right)
            value = term if value is None else value + term
        if "sum" not in once:
            once.add("sum")
            acc_buf[...] = value
        elif (ch, o) != LAST:
            acc_buf[...] += value
        else:
            fin_buf[...] = (acc_buf[...] + value).astype(BF16).reshape(fin_buf.shape)

    steps = dict(m=more, r=relay, c=compute, g=gates, p=pass_gates, n=gather_near, d=reduce, f=forward, j=project)
    for event in EVENTS:
        steps[event[0]](*[int(a) for a in event[1:]])

    def place(index):
        return out_ref.at[:, pl.ds(pl.multiple_of(index * columns, columns), columns)]

    for k in range(pairs - 1, -1, -1):
        for side in (1 - q, q) if k > 0 else (1 - q,):
            to = 2 * (nearest(p, k, pairs) if k > 0 else p) + side
            start(fin_buf.at[to], place(me), 4, fin_r, {"hist": to})
    keep = pltpu.make_async_copy(fin_buf.at[me], place(me), load_sem.at[6])
    keep.start()
    drained(gb.at[:3, 0, 0], 0)
    drained(hb, 3)

    @pl.when(p > 0)
    def _():
        drained(tb.at[2], 7)

    wx.wait_send()
    drained(send_buf, 9)
    drained(gb.at[0], 5)

    def share(n):
        return pl.ds(0, n * LANES)

    @pl.when(middle)
    def _():
        drained(gb.at[0], 6)
        drained(stage, 11)
        drained(stage, 12)
        drained(stage.at[:, 0], 13)
        drained(stage.at[0, 0], 14)
        if SLANT:
            drained(stage.at[:, 0, :, share(len(SLANT))], 15)

    @pl.when(jnp.logical_not(middle))
    def _():
        if DIRECT:
            drained(send_buf.at[0, :, share(len(DIRECT))], 10)
        for o in range(2):
            rest = len(widths) - sum(unit[1] == o for unit in SLANT)
            if rest:
                drained(gated.at[0, 0, :, :, share(rest)], 1 + o)

    drained(fin_buf.at[:total - 1], 4)
    keep.wait()
    arrived(out_ref.at[:, :(total - 1) * columns], fin_r)


def local_kernel(widths, history, filter_taps, gate_values, out_weight):
    rows, channels = history.shape
    owned = gate_values.shape[0]
    total = lax.axis_size("hist")
    cores = lax.axis_size("chan")
    pairs = total // 2
    tokens = owned * total
    quarter = channels // 4
    columns = out_weight.shape[1]
    part = owned // cores
    forward, inverse = tables(rows, tokens)
    forward = jnp.asarray(forward, F32).astype(BF16)
    inverse = jnp.asarray(inverse, F32).astype(BF16)
    dma = pltpu.SemaphoreType.DMA
    chunks = len(widths)
    each = dma((chunks,))
    scratch = [
        pltpu.VMEM((3, rows, quarter), BF16),
        pltpu.VMEM((2, 2, rows, quarter), BF16),
        pltpu.VMEM((pairs, 2, 2, owned, quarter), BF16),
        pltpu.VMEM((cores,) + out_weight.shape, BF16),
        pltpu.VMEM(forward.shape, BF16),
        pltpu.VMEM(inverse.shape, BF16),
        pltpu.VMEM((chunks, 2 * tokens, 2 * widths[0]), F32),
        pltpu.VMEM((2, tokens, quarter), BF16),
        pltpu.VMEM((2, tokens, quarter), F32),
        pltpu.VMEM((2, tokens, quarter), BF16),
        pltpu.VMEM((2, 2, tokens, quarter), BF16),
        pltpu.VMEM((cores, 2, tokens // cores, quarter), BF16),
        pltpu.VMEM((2, 2, cores, tokens // cores, quarter), BF16),
        pltpu.VMEM((tokens // cores, columns), F32),
        pltpu.VMEM((total, part, columns), BF16),
        dma((7,)), dma((16,)), each, each, each, each, dma, dma((3,)), dma,
        dma((chunks, 2)), dma((chunks, 2)), dma((chunks, 2)), dma((chunks, 2)), dma,
        pltpu.SemaphoreType.REGULAR((pairs - 2,)),
    ]
    return pl.pallas_call(
        functools.partial(kernel, pairs, widths),
        out_shape=jax.ShapeDtypeStruct((part, total * columns), BF16),
        in_specs=[pl.BlockSpec(memory_space=pl.ANY)] * 6,
        out_specs=pl.BlockSpec(memory_space=pl.ANY),
        scratch_shapes=scratch,
        compiler_params=pltpu.CompilerParams(
            collective_id=0, has_side_effects=True, vmem_limit_bytes=25165824
        ),
    )(*[pltpu.with_memory_space_constraint(x, pltpu.HBM) for x in (history, filter_taps, gate_values, out_weight, forward, inverse)])


def local(history, filter_taps, gate_values, out_weight):
    rows, channels = history.shape
    owned = gate_values.shape[0]
    total = lax.axis_size("hist")
    cores = lax.axis_size("chan")
    slabs = channels // (4 * LANES)
    fits = (
        total == 8
        and cores == 2
        and lax.axis_size("seq") == 2
        and owned % (16 * cores) == 0
        and rows == owned * total
        and channels % (4 * LANES) == 0
        and slabs == sum(PARTS)
        and out_weight.shape[1] % LANES == 0
    )
    if fits:
        widths = [LANES * part for part in PARTS]
        return local_kernel(widths, history, filter_taps, gate_values, out_weight)
    return local_general(history, filter_taps, gate_values, out_weight)


def solution(mesh):
    return jax.shard_map(
        local,
        mesh=mesh,
        in_specs=(
            P(("seq", "hist"), "chan"),
            P("hist", "chan"),
            P(("seq", "hist"), "chan"),
            P("chan", "hist"),
        ),
        out_specs=P(("seq", "hist", "chan"), None),
        check_vma=False,
    )
```
